32 devices in a mesh: ctx: 8 (over z, y), tp: 4 (over x, core).
Axes of the slice: x: 2, y: 2, z: 4, core: 2. Of those that a mesh axis runs over, the one named last changes fastest.
Arguments:
- hidden: bfloat16 [2, 2048, 1024], P(None, ('ctx', 'tp')), may hold values from -6 to 6
- w_qkv: bfloat16 [1024, 3, 1024], P('ctx', None, 'tp'), may hold values from -0.1875 to 0.1875
- w_attn_out: bfloat16 [1024, 1024], P('tp', 'ctx'), may hold values from -6 to 6
- w_in: bfloat16 [1024, 2, 2624], P('ctx', None, 'tp'), may hold values from -0.1875 to 0.1875
- w_mlp_out: bfloat16 [2624, 1024], P('tp', 'ctx'), may hold values from -0.125 to 0.125
- norm_attn: bfloat16 [1024], P('ctx'), may hold values from 0.25 to 1.75
- norm_mlp: bfloat16 [1024], P('ctx'), may hold values from 0.25 to 1.75
- out_grad: bfloat16 [2, 2048, 1024], P(None, ('ctx', 'tp')), may hold values from -6 to 6
Outputs:
- output: bfloat16 [2, 2048, 1024], P(None, ('ctx', 'tp'))
- d_hidden: float32 [2, 2048, 1024], P(None, ('ctx', 'tp'))
- d_w_qkv: float32 [1024, 3, 1024], P('ctx', None, 'tp')
- d_w_attn_out: float32 [1024, 1024], P('tp', 'ctx')
- d_w_in: float32 [1024, 2, 2624], P('ctx', None, 'tp')
- d_w_mlp_out: float32 [2624, 1024], P('tp', 'ctx')
- d_norm_attn: float32 [1024], P('ctx')
- d_norm_mlp: float32 [1024], P('ctx')
The draws below stay inside these ranges and needn't reach their ends.
All inputs are finite; a program needn't handle non-finite values.
Results may differ from the reference program's by a relative error of at most 0.023.
Values may be sent and summed in bfloat16 or wider, within the bound.
No kernel may reach another device: no remote copies, remote signals or barrier semaphores. Data moves between devices by JAX's collectives and lax.ppermute only.
A program may use at most 192 MiB of HBM per device.

```python
import math
import jax
import jax.numpy as jnp
from jax import lax

D = 1024
HEADS = 16
HEAD_DIM = 64
FF = 2624
MB = 2
SEQ = 2048


def raised(drawn, rng, source, target, shards_of, factor):
    def block_of(dim):
        return (jnp.arange(drawn.shape[dim]) // (drawn.shape[dim] // shards_of)).reshape((-1,) + (1,) * (drawn.ndim - 1 - dim))

    one_side = jax.random.permutation(rng, shards_of)[block_of(target)]
    far = (block_of(target) + shards_of // 2) % shards_of
    return jnp.where((block_of(source) == one_side) | (block_of(source) == far), factor * drawn, drawn)


def block_levels(stream_key, shape, pieces, least, high):
    level = 1.0
    for position, parts in pieces:
        draws = jax.random.uniform(jax.random.fold_in(jax.random.fold_in(stream_key, 6), position), (parts,), jnp.float32, least / len(pieces), high / len(pieces))
        level = level * jnp.repeat(jnp.exp(draws), shape[position] // parts).reshape((-1,) + (1,) * (len(shape) - 1 - position))
    return level


def noise(rng, shape, scale, bound, shards=(), kind=jnp.bfloat16):
    entries = scale * jax.random.normal(rng, shape, jnp.float32)
    if shards:
        entries = entries * block_levels(rng, shape, shards, -0.22, 0.18)
    return jnp.clip(entries, -bound, bound).astype(kind)


def heavy_noise(rng, dims, spread, most, shards, heavy, kind=jnp.bfloat16):
    values = spread * jax.random.normal(rng, dims, jnp.float32)
    if shards:
        values = values * block_levels(rng, dims, shards, -0.22, 0.18)
    return jnp.clip(raised(values, jax.random.fold_in(rng, 3), *heavy), -most, most).astype(kind)


def setup_inputs(seed: int = 0) -> dict:
    key_of = jax.random.split(jax.random.key(seed), 9)
    return {
        "hidden": noise(key_of[0], (MB, SEQ, D), 1.0, 6.0, ((1, 32),)),
        "w_qkv": noise(key_of[1], (D, 3, D), D ** -0.5, 0.1875, ((0, 8), (2, 4))),
        "w_attn_out": noise(key_of[2], (D, D), ((SEQ / (3 * D)) ** 0.5), 6.0, ((0, 4), (1, 8))),
        "w_in": noise(key_of[3], (D, 2, FF), D ** -0.5, 0.1875, ((0, 8), (2, 4))),
        "w_mlp_out": noise(key_of[4], (FF, D), FF ** -0.5, 0.125, ((0, 4), (1, 8))),
        "norm_attn": jnp.clip(1.0 + 0.15 * jax.random.normal(key_of[5], (D,), jnp.float32), 0.25, 1.75).astype(jnp.bfloat16),
        "norm_mlp": jnp.clip(1.0 + 0.15 * jax.random.normal(key_of[6], (D,), jnp.float32), 0.25, 1.75).astype(jnp.bfloat16),
        "out_grad": heavy_noise(key_of[7], (MB, SEQ, D), 1.0, 6.0, ((1, 32),), (1, 2, 32, 2.75)),
    }


@jax.custom_vjp
def low(v):
    return lax.optimization_barrier(v.astype(jnp.bfloat16)).astype(jnp.float32)

@jax.custom_vjp
def low_back(v):
    return v

def low_keep(v):
    return (low(v), None)

def low_pass(kept, grad):
    return (grad,)

def back_keep(v):
    return (v, None)

def back_low(kept, grad):
    return (low(grad),)
low.defvjp(low_keep, low_pass)
low_back.defvjp(back_keep, back_low)
highest = lax.Precision.HIGHEST

def normalize(values, gain):
    centred = values - lax.optimization_barrier(jnp.mean(values, axis=-1, keepdims=True))
    variance = lax.optimization_barrier(jnp.mean(centred * centred, axis=-1, keepdims=True))
    return centred * lax.rsqrt(variance + 1e-05) * gain

def rotate(values):
    middle = values.shape[-1] // 2
    return jnp.concatenate([-values[..., middle:], values[..., :middle]], axis=-1)

def rope_tables(positions):
    middle = HEAD_DIM // 2
    frequency = 160000.0 ** (-2.0 * jnp.arange(middle, dtype=jnp.float32) / HEAD_DIM)
    angles = positions.astype(jnp.float32)[:, None] * frequency[None, :]
    cosine = jnp.concatenate([jnp.cos(angles), jnp.cos(angles)], axis=1)[:, None, :]
    sine_part = jnp.concatenate([jnp.sin(angles), jnp.sin(angles)], axis=1)[:, None, :]
    return (cosine, sine_part)

def layer(inputs, w_qkv, w_attn_out, w_in, w_mlp_out, norm_attn, norm_mlp):
    length = inputs.shape[0]
    score_scale = 1.0 / math.sqrt(HEAD_DIM)
    cosine, sine_part = rope_tables(jnp.arange(length, dtype=jnp.int32))
    normed_one = low(normalize(inputs, norm_attn))
    qkv_rows = low_back(jnp.einsum('sd,dtf->stf', normed_one, w_qkv, precision=highest))
    queries = qkv_rows[:, 0].reshape(length, HEADS, HEAD_DIM)
    queries = low(queries * cosine + rotate(queries) * sine_part)
    keys_all = qkv_rows[:, 1].reshape(length, HEADS, HEAD_DIM)
    keys_all = low(keys_all * cosine + rotate(keys_all) * sine_part)
    value_rows = low(qkv_rows[:, 2].reshape(length, HEADS, HEAD_DIM))
    block_width = min(512, length)
    blocks = queries.reshape(length // block_width, block_width, HEADS, HEAD_DIM)

    def attend(query_block):
        scores = low_back(jnp.einsum('qhe,khe->hqk', query_block, keys_all, precision=highest) * score_scale)
        log_totals = jax.nn.logsumexp(scores, axis=2, keepdims=True)
        weights = low(jnp.exp(scores - log_totals))
        return jnp.einsum('hqk,khe->qhe', weights, value_rows, precision=highest)
    mixed_rows = lax.map(jax.checkpoint(attend), blocks).reshape(length, D)
    attended = low(low_back(mixed_rows))
    residual = inputs + low_back(jnp.dot(attended, w_attn_out, precision=highest))
    normed_two = low(normalize(residual, norm_mlp))
    gate_up = low_back(jnp.einsum('sd,dtf->stf', normed_two, w_in, precision=highest))
    product = low(jax.nn.gelu(gate_up[:, 0], approximate=False) * gate_up[:, 1])
    return residual + low_back(jnp.dot(product, w_mlp_out, precision=highest))

def reference(hidden, w_qkv, w_attn_out, w_in, w_mlp_out, norm_attn, norm_mlp, out_grad):
    weight_qkv = w_qkv.astype(jnp.float32)
    weight_out = w_attn_out.astype(jnp.float32)
    weight_in = w_in.astype(jnp.float32)
    weight_mlp = w_mlp_out.astype(jnp.float32)
    gain_attn = norm_attn.astype(jnp.float32)
    gain_mlp = norm_mlp.astype(jnp.float32)

    def one_sequence(totals, inputs_pair):
        sequence, cotangent = inputs_pair
        result, pull_back = jax.vjp(layer, sequence.astype(jnp.float32), weight_qkv, weight_out, weight_in, weight_mlp, gain_attn, gain_mlp)
        grads = pull_back(cotangent.astype(jnp.float32))
        new_totals = tuple((total + grad for total, grad in zip(totals, grads[1:])))
        return (new_totals, (result.astype(jnp.bfloat16), grads[0]))
    start = (jnp.zeros(w_qkv.shape, jnp.float32), jnp.zeros(w_attn_out.shape, jnp.float32), jnp.zeros(w_in.shape, jnp.float32), jnp.zeros(w_mlp_out.shape, jnp.float32), jnp.zeros(norm_attn.shape, jnp.float32), jnp.zeros(norm_mlp.shape, jnp.float32))
    totals, stacked = lax.scan(one_sequence, start, (hidden, out_grad))
    return (stacked[0], stacked[1], totals[0], totals[1], totals[2], totals[3], totals[4], totals[5])
```

```python
import functools
import math

import jax
import jax.numpy as jnp
from jax import lax
from jax.experimental import pallas as pl
from jax.experimental.pallas import tpu as pltpu
from jax.sharding import PartitionSpec as P

HEAD_DIM = 64


epsilon = 1e-05


def normalize(values):
    centred = values - jnp.mean(values, axis=-1, keepdims=True)
    inverse = lax.rsqrt(jnp.mean(centred * centred, axis=-1, keepdims=True) + epsilon)
    return (centred * inverse, inverse)


def norm_back(grad_normed, normed, inverse, gain):
    scaled = grad_normed * gain
    return inverse * (
        scaled
        - jnp.mean(scaled, axis=-1, keepdims=True)
        - normed * jnp.mean(scaled * normed, axis=-1, keepdims=True)
    )


def rotate(values):
    middle = values.shape[-1] // 2
    return jnp.concatenate([-values[..., middle:], values[..., :middle]], axis=-1)


def unrotate(values):
    middle = values.shape[-1] // 2
    return jnp.concatenate([values[..., middle:], -values[..., :middle]], axis=-1)


def rope_tables(positions):
    middle = HEAD_DIM // 2
    frequency = 160000.0 ** (-2.0 * jnp.arange(middle, dtype=jnp.float32) / HEAD_DIM)
    angles = positions.astype(jnp.float32)[:, None] * frequency[None, :]
    cosine = jnp.concatenate([jnp.cos(angles), jnp.cos(angles)], axis=1)[:, None, :]
    sine_part = jnp.concatenate([jnp.sin(angles), jnp.sin(angles)], axis=1)[:, None, :]
    return (cosine, sine_part)


def gelu_exact(values):
    return jax.nn.gelu(values, approximate=False)


def score_tile(queries, keys_block):
    score_scale = 1.0 / math.sqrt(HEAD_DIM)
    return (
        jnp.einsum("qhe,khe->hqk", queries, keys_block, preferred_element_type=jnp.float32)
        * score_scale
    )


def key_totals(queries, everywhere):
    block_rows, heads_here, head_size = queries.shape

    def absorb(running, keys_block):
        running_max, running_sum = running
        scores = score_tile(queries, keys_block.reshape(block_rows, heads_here, head_size))
        raised = jnp.maximum(running_max, jnp.max(scores, axis=2))
        running_sum = running_sum * jnp.exp(running_max - raised) + jnp.sum(
            jnp.exp(scores - raised[..., None]), axis=2
        )
        return (raised, running_sum)

    start = (
        jnp.full((heads_here, block_rows), -1e30, jnp.float32),
        jnp.zeros((heads_here, block_rows), jnp.float32),
    )

    def tile_turn(tile_index, running):
        tile = lax.dynamic_slice_in_dim(everywhere[0], tile_index * block_rows, block_rows, 0)
        return absorb(running, tile)

    running_max, running_sum = lax.fori_loop(0, lax.axis_size("ctx"), tile_turn, start)
    return running_max + jnp.log(running_sum)


def attend(queries, log_totals, everywhere):
    block_rows, heads_here, head_size = queries.shape

    def absorb(summed, pair_block):
        keys_block = pair_block[0].reshape(block_rows, heads_here, head_size)
        value_block = pair_block[1].reshape(block_rows, heads_here, head_size)
        weights = jnp.exp(score_tile(queries, keys_block) - log_totals[..., None]).astype(
            jnp.bfloat16
        )
        return summed + jnp.einsum(
            "hqk,khe->qhe", weights, value_block, preferred_element_type=jnp.float32
        )

    start = jnp.zeros(queries.shape, jnp.float32)

    def tile_turn(tile_index, summed):
        tile = lax.dynamic_slice_in_dim(everywhere, tile_index * block_rows, block_rows, 1)
        return absorb(summed, tile)

    summed = lax.fori_loop(0, lax.axis_size("ctx"), tile_turn, start)
    return summed


def attend_back(queries, key_pair, log_totals, grad_out, offset, everywhere):
    block_rows, heads_here, head_size = queries.shape
    score_scale = 1.0 / math.sqrt(HEAD_DIM)

    def absorb(pair_block, key_grads, grad_query):
        keys_block = pair_block[0].reshape(block_rows, heads_here, head_size)
        value_block = pair_block[1].reshape(block_rows, heads_here, head_size)
        weights = jnp.exp(score_tile(queries, keys_block) - log_totals[..., None])
        grad_weights = jnp.einsum(
            "qhe,khe->hqk", grad_out, value_block, preferred_element_type=jnp.float32
        )
        grad_scores = (weights * (grad_weights - offset[..., None])).astype(jnp.bfloat16)
        grad_query = (
            grad_query
            + jnp.einsum(
                "hqk,khe->qhe", grad_scores, keys_block, preferred_element_type=jnp.float32
            )
            * score_scale
        )
        grad_keys = (
            jnp.einsum("hqk,qhe->khe", grad_scores, queries, preferred_element_type=jnp.float32)
            * score_scale
        )
        grad_values = jnp.einsum(
            "hqk,qhe->khe",
            weights.astype(jnp.bfloat16),
            grad_out,
            preferred_element_type=jnp.float32,
        )
        key_grads = jnp.stack(
            [grad_keys.reshape(block_rows, -1), grad_values.reshape(block_rows, -1)]
        )
        return (key_grads, grad_query)

    def tile_turn(tile_index, carried):
        all_grads, grad_query = carried
        tile = lax.dynamic_slice_in_dim(everywhere, tile_index * block_rows, block_rows, 1)
        tile_grads, grad_query = absorb(tile, jnp.zeros(key_pair.shape, jnp.float32), grad_query)
        all_grads = lax.dynamic_update_slice_in_dim(
            all_grads, tile_grads, tile_index * block_rows, 1
        )
        return (all_grads, grad_query)

    start = (jnp.zeros(everywhere.shape, jnp.float32), jnp.zeros(queries.shape, jnp.float32))
    all_grads, grad_query = lax.fori_loop(0, lax.axis_size("ctx"), tile_turn, start)
    owned = lax.psum_scatter(all_grads, "ctx", scatter_dimension=1, tiled=True)
    return (owned, grad_query)


def to_block(local_part):
    return lax.all_gather(local_part, "tp", axis=0, tiled=True)


def grad_block(local_part):
    return lax.all_gather(local_part, "tp", axis=0, tiled=True)


def project_rows(operand, weight):
    return lax.psum_scatter(
        jnp.dot(operand, weight, preferred_element_type=jnp.float32).astype(jnp.bfloat16),
        "tp",
        scatter_dimension=0,
        tiled=True,
    ).astype(jnp.float32)


def sum_rows(grad_parts, weight):
    return lax.psum_scatter(
        jnp.einsum("stf,dtf->sd", grad_parts, weight, preferred_element_type=jnp.float32).astype(
            jnp.bfloat16
        ),
        "tp",
        scatter_dimension=0,
        tiled=True,
    ).astype(jnp.float32)


def on_device(hidden, w_qkv, w_attn_out, w_in, w_mlp_out, norm_attn, norm_mlp, out_grad):
    ctx_count = lax.axis_size("ctx")
    local_rows = hidden.shape[1]
    block_rows = local_rows * lax.axis_size("tp")
    heads_here = w_qkv.shape[2] // HEAD_DIM
    positions = lax.axis_index("ctx") * block_rows + jnp.arange(block_rows, dtype=jnp.int32)
    cosine, sine_part = rope_tables(positions)
    acc_qkv = jnp.zeros((w_qkv.shape[0] * ctx_count, w_qkv.shape[1], w_qkv.shape[2]), jnp.float32)
    acc_out = jnp.zeros((w_attn_out.shape[0], w_attn_out.shape[1] * ctx_count), jnp.float32)
    acc_in = jnp.zeros((w_in.shape[0] * ctx_count, w_in.shape[1], w_in.shape[2]), jnp.float32)
    acc_mlp = jnp.zeros((w_mlp_out.shape[0], w_mlp_out.shape[1] * ctx_count), jnp.float32)
    acc_gain_attn = jnp.zeros((norm_attn.shape[0] * ctx_count,), jnp.float32)
    acc_gain_mlp = jnp.zeros((norm_mlp.shape[0] * ctx_count,), jnp.float32)
    outputs = []
    input_grads = []
    for micro_index in range(hidden.shape[0]):
        gathered = (
            lax.all_gather(w_qkv, "ctx", axis=0, tiled=True),
            lax.all_gather(w_attn_out, "ctx", axis=1, tiled=True),
            lax.all_gather(w_in, "ctx", axis=0, tiled=True),
            lax.all_gather(w_mlp_out, "ctx", axis=1, tiled=True),
            lax.all_gather(norm_attn, "ctx", axis=0, tiled=True),
            lax.all_gather(norm_mlp, "ctx", axis=0, tiled=True),
        )
        full_qkv, full_out, full_in, full_mlp, gain_attn, gain_mlp = gathered
        gain_attn = gain_attn.astype(jnp.float32)
        gain_mlp = gain_mlp.astype(jnp.float32)
        input_rows = hidden[micro_index].astype(jnp.float32)
        normed_one, inverse_one = normalize(input_rows)
        first_block = to_block((normed_one * gain_attn).astype(jnp.bfloat16))
        qkv_rows = jnp.einsum(
            "sd,dtf->stf", first_block, full_qkv, preferred_element_type=jnp.float32
        )
        raw_queries = qkv_rows[:, 0].reshape(block_rows, heads_here, HEAD_DIM)
        queries = (raw_queries * cosine + rotate(raw_queries) * sine_part).astype(jnp.bfloat16)
        raw_keys = qkv_rows[:, 1].reshape(block_rows, heads_here, HEAD_DIM)
        keys_here = (
            (raw_keys * cosine + rotate(raw_keys) * sine_part)
            .astype(jnp.bfloat16)
            .reshape(block_rows, -1)
        )
        values_here = qkv_rows[:, 2].astype(jnp.bfloat16)
        key_pair = jnp.stack([keys_here, values_here])
        everywhere = lax.all_gather(key_pair, "ctx", axis=1, tiled=True)
        log_totals = key_totals(queries, everywhere)
        attended = attend(queries, log_totals, everywhere).reshape(block_rows, -1)
        attended_low = attended.astype(jnp.bfloat16)
        residual = input_rows + project_rows(attended_low, full_out)
        normed_two, inverse_two = normalize(residual)
        second_block = to_block((normed_two * gain_mlp).astype(jnp.bfloat16))
        gate_up = jnp.einsum(
            "sd,dtf->stf", second_block, full_in, preferred_element_type=jnp.float32
        )
        activated, gelu_pull = jax.vjp(gelu_exact, gate_up[:, 0])
        product = (activated * gate_up[:, 1]).astype(jnp.bfloat16)
        result = residual + project_rows(product, full_mlp)
        outputs.append(result.astype(jnp.bfloat16))
        cotangent_block = grad_block(out_grad[micro_index])
        grad_act = jnp.einsum(
            "sd,fd->sf", cotangent_block, full_mlp, preferred_element_type=jnp.float32
        )
        acc_mlp = acc_mlp + jnp.einsum(
            "sf,sd->fd", product, cotangent_block, preferred_element_type=jnp.float32
        )
        grad_gate = gelu_pull(grad_act * gate_up[:, 1])[0]
        grad_gate_up = jnp.stack([grad_gate, grad_act * activated], axis=1).astype(jnp.bfloat16)
        acc_in = acc_in + jnp.einsum(
            "sd,stf->dtf", second_block, grad_gate_up, preferred_element_type=jnp.float32
        )
        grad_two = sum_rows(grad_gate_up, full_in)
        acc_gain_mlp = acc_gain_mlp + jnp.sum(grad_two * normed_two, axis=0)
        grad_residual = out_grad[micro_index].astype(jnp.float32) + norm_back(
            grad_two, normed_two, inverse_two, gain_mlp
        )
        attn_block = grad_block(grad_residual.astype(jnp.bfloat16))
        grad_mixed = jnp.einsum(
            "sd,fd->sf", attn_block, full_out, preferred_element_type=jnp.float32
        ).astype(jnp.bfloat16)
        acc_out = acc_out + jnp.einsum(
            "sf,sd->fd", attended_low, attn_block, preferred_element_type=jnp.float32
        )
        grad_heads = grad_mixed.reshape(block_rows, heads_here, HEAD_DIM)
        offset = jnp.sum(
            grad_heads.astype(jnp.float32) * attended.reshape(block_rows, heads_here, HEAD_DIM),
            axis=2,
        ).T
        pair_grads, grad_query = attend_back(
            queries, key_pair, log_totals, grad_heads, offset, everywhere
        )
        grad_keys = pair_grads[0].reshape(block_rows, heads_here, HEAD_DIM)
        grad_q_raw = (grad_query * cosine + unrotate(grad_query * sine_part)).reshape(
            block_rows, -1
        )
        grad_k_raw = (grad_keys * cosine + unrotate(grad_keys * sine_part)).reshape(block_rows, -1)
        grad_qkv = jnp.stack([grad_q_raw, grad_k_raw, pair_grads[1]], axis=1).astype(jnp.bfloat16)
        acc_qkv = acc_qkv + jnp.einsum(
            "sd,stf->dtf", first_block, grad_qkv, preferred_element_type=jnp.float32
        )
        grad_one = sum_rows(grad_qkv, full_qkv)
        acc_gain_attn = acc_gain_attn + jnp.sum(grad_one * normed_one, axis=0)
        input_grads.append(grad_residual + norm_back(grad_one, normed_one, inverse_one, gain_attn))
    summed = (
        lax.psum_scatter(acc_qkv, "ctx", scatter_dimension=0, tiled=True),
        lax.psum_scatter(acc_out, "ctx", scatter_dimension=1, tiled=True),
        lax.psum_scatter(acc_in, "ctx", scatter_dimension=0, tiled=True),
        lax.psum_scatter(acc_mlp, "ctx", scatter_dimension=1, tiled=True),
        lax.psum_scatter(acc_gain_attn, "ctx", scatter_dimension=0, tiled=True),
        lax.psum_scatter(acc_gain_mlp, "ctx", scatter_dimension=0, tiled=True),
    )
    gain_sums = lax.psum((summed[4], summed[5]), "tp")
    return (
        jnp.stack(outputs),
        jnp.stack(input_grads),
        summed[0],
        summed[1],
        summed[2],
        summed[3],
        gain_sums[0],
        gain_sums[1],
    )


def normed(values):
    centred = values - jnp.mean(values, axis=-1, keepdims=True)
    inverse = lax.rsqrt(jnp.mean(centred * centred, axis=-1, keepdims=True) + epsilon)
    return centred * inverse, inverse


def back_normed(scaled, values):
    unit, inverse = normed(values)
    return inverse * (
        scaled
        - jnp.mean(scaled, axis=-1, keepdims=True)
        - unit * jnp.mean(scaled * unit, axis=-1, keepdims=True)
    )


def f32(values):
    return values.astype(jnp.float32)


def low(values):
    return values.astype(jnp.bfloat16)


def mm(left, right):
    return jnp.dot(left, right, preferred_element_type=jnp.float32)


def mm_nt(left, right):
    return lax.dot_general(
        left, right, (((1,), (1,)), ((), ())), preferred_element_type=jnp.float32
    )


def mm_tn(left, right):
    return lax.dot_general(
        left, right, (((0,), (0,)), ((), ())), preferred_element_type=jnp.float32
    )


def local_call(kernel, outs, ids, *arrays, scratch=(), flops=0, name=None):
    moved = sum(math.prod(a.shape) * a.dtype.itemsize for a in (*arrays, *outs))
    return pl.pallas_call(
        kernel,
        out_shape=tuple(outs),
        in_specs=[pl.BlockSpec(memory_space=pltpu.SMEM)]
        + [pl.BlockSpec(memory_space=pltpu.VMEM)] * len(arrays),
        out_specs=tuple(pl.BlockSpec(memory_space=pltpu.VMEM) for _ in outs),
        scratch_shapes=list(scratch),
        cost_estimate=pl.CostEstimate(flops=flops, bytes_accessed=moved, transcendentals=0),
        compiler_params=pltpu.CompilerParams(vmem_limit_bytes=60 << 20),
        name=name,
    )(ids, *arrays)


def shaped(shape, kind=jnp.bfloat16):
    return jax.ShapeDtypeStruct(shape, kind)


def ring_order(count):
    return list(range(0, count, 2)) + list(range(count - 1, 0, -2))


def aligned(index, size):
    return pl.multiple_of(index * size, size)


CTX, LOW, HIGH, RING = 0, 1, 2, 3


def first_kernel(ids, hidden, kept, sent):
    for out, index in ((kept, ids[LOW]), (sent, 1 - ids[LOW])):
        unit, _ = normed(f32(hidden[index]))
        out[...] = low(unit)


def order_kernel(ids, hidden, cotangent, hidden_out, cotangent_out):
    width = hidden.shape[2] // 8
    rows = hidden.shape[1]
    for m in range(2):
        for j in range(8):
            block = pl.ds(aligned(ids[RING + j], width), width)
            where = (pl.ds(m * rows, rows), pl.ds(j * width, width))
            hidden_out[where] = hidden[ids[LOW] ^ m, :, block]
            cotangent_out[where] = cotangent[ids[LOW] ^ m, :, block]


def head_kernel(ids, w_qkv, gain_column, *outs):
    half = w_qkv.shape[1] // 2
    scaled = [low(f32(w_qkv[t]) * gain_column[...]) for t in range(3)]
    for rel, out in enumerate(outs):
        head = ids[HIGH] ^ rel
        parts = []
        for t in range(3):
            part = scaled[t][:, :HEAD_DIM]
            for h in range(1, 4):
                part = jnp.where(head == h, scaled[t][:, h * HEAD_DIM : (h + 1) * HEAD_DIM], part)
            parts.append(part)
        out[: 2 * half] = jnp.concatenate(parts[:2], axis=1)
        out[2 * half :] = jnp.concatenate([parts[2][:half], parts[2][half:]], axis=1)


def swap_halves(values):
    lane = lax.broadcasted_iota(jnp.int32, values.shape, 1)
    return jnp.where(
        lane % HEAD_DIM < HEAD_DIM // 2,
        pltpu.roll(values, 128 - HEAD_DIM // 2, 1),
        pltpu.roll(values, HEAD_DIM // 2, 1),
    )


def tile_tables(slot, cos_a, sin_a, cos_b, sin_b):
    cosines, sines = [], []
    for s in range(4):
        row = pl.ds(slot * 4 + s, 1)
        ca, sa = cos_a[row], sin_a[row]
        cosines.append(ca * cos_b[...] - sa * sin_b[...])
        sines.append(sa * cos_b[...] + ca * sin_b[...])
    lane = lax.broadcasted_iota(jnp.int32, (1, 128), 1)
    sign = jnp.where(lane % HEAD_DIM < HEAD_DIM // 2, -1.0, 1.0)
    return jnp.concatenate(cosines, 0), jnp.concatenate(sines, 0) * sign


def as_row(column):
    return jnp.transpose(jnp.broadcast_to(column, (column.shape[0], 128)))[:8]


def packed(values):
    half = values.shape[0] // 2
    return jnp.concatenate([values[:half], values[half:]], axis=1)


def unpacked(values):
    return jnp.concatenate([values[:, :HEAD_DIM], values[:, HEAD_DIM:]], axis=0)


def forward_kernel(ids, *refs):
    tokens, heads, tables = refs[:32], refs[32:40], refs[40:44]
    outs, (qk_out, v_out, o_out, lse_out) = refs[44:52], refs[52:56]
    weight, key_all = refs[56:]
    half = heads[0].shape[0] // 3
    for k in range(8):
        start = aligned(ids[CTX] ^ k, 2 * half)
        weight[pl.ds(start, 2 * half), :128] = heads[k][: 2 * half]
        weight[pl.ds(start, half), 128:] = heads[k][2 * half :, :HEAD_DIM]
        weight[pl.ds(start + half, half), 128:] = heads[k][2 * half :, HEAD_DIM:]
    size = qk_out.shape[1]
    lane = lax.broadcasted_iota(jnp.int32, (1, 128), 1)
    scale = jnp.where(lane < HEAD_DIM, 1.0 / math.sqrt(HEAD_DIM), 1.0)
    for k in range(8):
        rows = jnp.concatenate([tokens[4 * k + s][...] for s in range(4)], axis=0)
        made = mm(rows, weight[...])
        cosine, sine = tile_tables(k, *tables)
        turned = made[:, :128]
        turned = low((turned * cosine + swap_halves(turned) * sine) * scale)
        qk_out[k] = turned
        key_all[pl.ds(k * size, size)] = turned[:, HEAD_DIM:]
        v_out[pl.ds(k * size, size)] = low(made[:, 128:])

    def tile(k, _):
        scores = mm_nt(qk_out[k][:, :HEAD_DIM], key_all[...])
        top = jnp.max(scores, axis=1, keepdims=True)
        raised = jnp.exp(scores - top)
        total = jnp.sum(raised, axis=1, keepdims=True)
        o_out[k] = mm(low(raised), v_out[...]) / total
        lse_out[k] = as_row(top + jnp.log(total))
        return 0

    lax.fori_loop(0, 8, tile, 0)
    for k in range(8):
        outs[k][...] = low(packed(o_out[k]))


def heads_to_rows(ids, pieces, columns):
    del columns
    return pieces


def out_kernel(ids, *refs):
    pieces, weights = refs[:8], refs[8:16]
    kept, sent, att_out = refs[16:19]
    stage = refs[19]
    rows = pieces[0].shape[0] // 2
    for k in range(8):
        m, rel = k & 1, k >> 1
        for half in range(2):
            for s in range(2):
                at = pl.ds(half * 4 * rows + s * 2 * rows + m * rows, rows)
                stage[rel, at] = pieces[k][s * rows : (s + 1) * rows, half * HEAD_DIM : (half + 1) * HEAD_DIM]
    att = jnp.concatenate([stage[ids[HIGH] ^ h] for h in range(4)], axis=1)
    att_out[...] = att
    weight = jnp.concatenate([w[...] for w in weights], axis=1)
    made = low(mm(att, weight))
    kept[...] = made[: 4 * rows]
    sent[...] = made[4 * rows :]


def sum_kernel(ids, kept, got, out):
    out[...] = low(f32(kept[...]) + f32(got[...]))


def swapped(values):
    half = values.shape[0] // 2
    return jnp.concatenate([values[half:], values[:half]], axis=0)


def second_kernel(ids, own, other, mine, got, residual_out, normed_out):
    residual = jnp.concatenate([f32(own[...]), f32(other[...])], axis=0)
    residual = residual + (f32(mine[...]) + swapped(f32(got[...])))
    residual_out[...] = residual
    normed_out[...] = low(normed(residual)[0])


def mlp_kernel(ids, rows, cot_a, cot_b, w_in, w_out, result, back, act_out, grad_out):
    width = w_out.shape[0]
    tokens = rows[...]
    cotangent = jnp.concatenate([cot_a[...], cot_b[...]], axis=0)
    gate = mm_nt(tokens, w_in[:width])
    cumulative = 0.5 + 0.5 * lax.erf(gate * math.sqrt(0.5))
    density = jnp.exp(-0.5 * gate * gate) * (1.0 / math.sqrt(2.0 * math.pi))
    active = gate * cumulative
    up = mm_nt(tokens, w_in[width:])
    product = low(active * up)
    act_out[...] = product
    grad_act = mm_nt(cotangent, w_out[...])
    grad_gate = low(grad_act * up * (cumulative + gate * density))
    grad_up = low(grad_act * active)
    grad_out[:, :width] = grad_gate
    grad_out[:, width:] = grad_up
    back[...] = low(mm(grad_gate, w_in[:width]) + mm(grad_up, w_in[width:]))
    result[...] = low(mm(product, w_out[...]))


def weight_kernel(groups, ids, *refs):
    ins, outs = refs[: -9], refs[-9:]
    base = 0
    at = 0
    top = outs[4].shape[0]
    for left_count, right_count in groups:
        left = jnp.concatenate([r[...] for r in ins[at : at + left_count]], axis=0)
        at += left_count
        right = jnp.concatenate([r[...] for r in ins[at : at + right_count]], axis=0)
        at += right_count
        made = low(mm_tn(left, right))
        size = made.shape[0]
        for j in range(8):
            block = made[:, j * 128 : (j + 1) * 128]
            if j != 4:
                outs[j if j < 4 else j + 1][base : base + size] = block
                continue
            cut = min(max(top - base, 0), size)
            if cut:
                outs[4][base : base + cut] = block[:cut]
            if cut < size:
                start = base + cut - top
                outs[5][start : start + size - cut] = block[cut:]
        base += size


def third_kernel(ids, cot_a, cot_b, mine, got, residual, grad_out, low_out):
    scaled = f32(mine[...]) + swapped(f32(got[...]))
    cotangent = jnp.concatenate([f32(cot_a[...]), f32(cot_b[...])], axis=0)
    grad = cotangent + back_normed(scaled, residual[...])
    grad_out[...] = grad[: grad_out.shape[0]]
    low_out[...] = low(grad)


def grad_heads_kernel(ids, grad_a, grad_b, *refs):
    weights, outs = refs[:8], refs[8:]
    grads = jnp.concatenate([grad_a[...], grad_b[...]], axis=0)
    made = sum(
        mm_nt(
            grads[:, j * 128 : (j + 1) * 128],
            jnp.concatenate(
                [weights[j][pl.ds(aligned(ids[HIGH] ^ rel, HEAD_DIM), HEAD_DIM)] for rel in range(4)],
                axis=0,
            ),
        )
        for j in range(8)
    )
    made = low(made)
    rows = made.shape[0] // 8
    for k in range(8):
        m, rel = k & 1, k >> 1
        sides = []
        for half in range(2):
            sides.append(
                jnp.concatenate(
                    [
                        made[
                            half * 4 * rows + s * 2 * rows + m * rows : half * 4 * rows + s * 2 * rows + (m + 1) * rows,
                            rel * HEAD_DIM : (rel + 1) * HEAD_DIM,
                        ]
                        for s in range(2)
                    ],
                    axis=0,
                )
            )
        outs[k][...] = jnp.concatenate(sides, axis=1)


def backward_kernel(ids, *refs):
    grads, (qk, value, o_in, lse), tables = refs[:8], refs[8:12], refs[12:16]
    outs = refs[16:24]
    key_all, grad_all, grad_q, grad_k, grad_v = refs[24:]
    size = qk.shape[1]
    for k in range(8):
        key_all[pl.ds(k * size, size)] = qk[k][:, HEAD_DIM:]
        grad_all[k] = unpacked(grads[k][...])
    grad_k[...] = jnp.zeros(grad_k.shape, jnp.float32)
    grad_v[...] = jnp.zeros(grad_v.shape, jnp.float32)

    def tile(k, _):
        query = qk[k][:, :HEAD_DIM]
        grad = grad_all[k]
        offset = as_row(jnp.sum(f32(grad) * o_in[k], axis=1, keepdims=True))[:1]
        weights = jnp.exp(mm_nt(key_all[...], query) - lse[k][:1])
        grad_scores = low(weights * (mm_nt(value[...], grad) - offset))
        grad_v[...] += mm(low(weights), grad)
        grad_k[...] += mm(grad_scores, query)
        grad_q[k] = mm_tn(grad_scores, key_all[...])
        return 0

    lax.fori_loop(0, 8, tile, 0)
    scale = 1.0 / math.sqrt(HEAD_DIM)
    for k in range(8):
        at = pl.ds(k * size, size)
        cosine, sine = tile_tables(k, *tables)
        pair = jnp.concatenate([grad_q[k] * scale, grad_k[at]], axis=1)
        outs[k][:size] = low(pair * cosine - swap_halves(pair) * sine)
        outs[k][size:] = low(packed(grad_v[at]))


def head_grad_kernel(ids, *refs):
    tokens, grads, outs, total = refs[:32], refs[32:40], refs[40:48], refs[48]
    size = grads[0].shape[0] * 2 // 3
    pair_rows = jnp.concatenate([g[:size] for g in grads], axis=0)
    value_rows = jnp.concatenate([unpacked(g[size:]) for g in grads], axis=0)
    rows = jnp.concatenate([t[...] for t in tokens], axis=0)
    total[:128] = mm_tn(pair_rows, rows)
    total[128:] = mm_tn(value_rows, rows)
    for k in range(8):
        outs[k][...] = low(total[:, pl.ds(aligned(ids[CTX] ^ k, 128), 128)])


def back_kernel(ids, *refs):
    grads, weights = refs[:8], refs[8:16]
    kept, sent, stage = refs[16:]
    size = grads[0].shape[0] * 2 // 3
    rows = size // 4
    for k in range(8):
        m, rel = k & 1, k >> 1
        for half in range(2):
            for s in range(2):
                at = pl.ds(half * 4 * rows + s * 2 * rows + m * rows, rows)
                source = half * 2 * rows + s * rows
                pair = grads[k][source : source + rows]
                stage[0, rel, at] = pair[:, :HEAD_DIM]
                stage[1, rel, at] = pair[:, HEAD_DIM:]
                stage[2, rel, at] = grads[k][
                    size + s * rows : size + (s + 1) * rows, half * HEAD_DIM : (half + 1) * HEAD_DIM
                ]
    parts = [
        jnp.concatenate([stage[t, ids[HIGH] ^ h] for h in range(4)], axis=1) for t in range(3)
    ]
    for j in range(8):
        made = low(sum(mm_nt(parts[t], weights[j][t]) for t in range(3)))
        kept[:, j * 128 : (j + 1) * 128] = made[: 4 * rows]
        sent[:, j * 128 : (j + 1) * 128] = made[4 * rows :]


def store_blocks(ids, out, values):
    width = out.shape[2] // 8
    rows = out.shape[1]
    for m in range(2):
        for j in range(8):
            out[ids[LOW] ^ m, :, pl.ds(aligned(ids[RING + j], width), width)] = values[
                m * rows : (m + 1) * rows, j * width : (j + 1) * width
            ].astype(out.dtype)


def output_kernel(ids, residual, mine, got, out):
    store_blocks(ids, out, residual[...] + (f32(mine[...]) + f32(got[...])))


def last_kernel(ids, grad, own, mine, got, out):
    scaled = f32(mine[...]) + f32(got[...])
    store_blocks(ids, out, grad[...] + back_normed(scaled, f32(own[...])))


def columns_kernel(ids, *refs):
    pieces, gain, weight = refs[:8], refs[8], refs[9]
    grad_out, gain_out, stage = refs[10:]
    for rel in range(4):
        stage[rel] = jnp.transpose(f32(pieces[2 * rel][...]) + f32(pieces[2 * rel + 1][...]))
    gains = jnp.zeros(gain_out.shape, jnp.float32)
    for t in range(3):
        part = jnp.concatenate(
            [stage[ids[HIGH] ^ h][:, t * HEAD_DIM : (t + 1) * HEAD_DIM] for h in range(4)], axis=1
        )
        gains = gains + jnp.sum(part * f32(weight[t]), axis=1, keepdims=True)
        grad_out[t] = part * gain[...]
    gain_out[...] = gains


def fast_layer(hidden, w_qkv, w_attn_out, w_in, w_mlp_out, norm_attn, norm_mlp, out_grad):
    count = lax.axis_size("ctx")
    order = ring_order(count)
    place = [order.index(c) for c in range(count)]
    rows = hidden.shape[1]
    width = hidden.shape[2]
    units = w_mlp_out.shape[0]
    ctx, tp = lax.axis_index("ctx"), lax.axis_index("tp")
    table = jnp.array(
        [
            [c, c & 1, c >> 1] + [order[(place[c] + j) % count] for j in range(count)]
            for c in range(count)
        ],
        jnp.int32,
    )
    ids = lax.dynamic_index_in_dim(table, ctx, 0, keepdims=False)

    def across(values, bits):
        return lax.ppermute(values, "ctx", [(i, i ^ bits) for i in range(count)])

    def beside(values, bits):
        return lax.ppermute(values, "tp", [(i, i ^ bits) for i in range(4)])

    def turn(values, step):
        return lax.ppermute(
            values, "ctx", [(order[i], order[(i + step) % count]) for i in range(count)]
        )

    core, side = 1, 2

    def ring_gather(part):
        ahead, behind = [part], [part]
        for _ in range(3):
            behind.append(turn(behind[-1], 1))
            ahead.append(turn(ahead[-1], -1))
        cut = part.shape[-2] // 32 * 16
        if part.ndim == 2:
            far = jnp.concatenate([turn(behind[3][:cut], 1), turn(ahead[3][cut:], -1)], axis=0)
        else:
            far = jnp.concatenate([turn(behind[3][:, :cut], 1), turn(ahead[3][:, cut:], -1)], axis=1)
        return ahead + [far] + behind[:0:-1]

    def ring_sum(blocks):
        near, top, bottom, rest = blocks[:4], blocks[4], blocks[5], blocks[6:]
        cut = top.shape[0]
        right, left = turn(top, 1), turn(bottom, -1)
        right = jnp.concatenate([low(f32(near[3][:cut]) + f32(right)), near[3][cut:]], axis=0)
        left = jnp.concatenate([rest[0][:cut], low(f32(rest[0][cut:]) + f32(left))], axis=0)
        for step in (2, 1):
            right, left = turn(right, 1), turn(left, -1)
            right = low(f32(near[step]) + f32(right))
            left = low(f32(rest[3 - step]) + f32(left))
        return near[0], turn(right, 1), turn(left, -1)

    kept, sent = local_call(first_kernel, [shaped((rows, width))] * 2, ids, hidden, name="first")
    gain_one = f32(norm_attn)
    gain_two = f32(norm_mlp)
    w_qkv_rows = jnp.transpose(w_qkv, (1, 0, 2))
    pieces = local_call(
        head_kernel,
        [shaped((192, 128))] * 4,
        ids,
        w_qkv_rows,
        gain_one[:, None],
        name="head_weights",
    )
    heads = [pieces[0]] + [across(pieces[k >> 1], k) for k in range(1, 8)]
    near = [kept] + [across(kept if k % 2 == 0 else sent, k) for k in range(1, 8)]
    tokens = []
    for k in range(8):
        beyond = beside(near[k], side)
        tokens += [near[k], beyond, beside(near[k], core), beside(beyond, core)]

    frequency = 160000.0 ** (
        -2.0 * (jnp.arange(128, dtype=jnp.int32) % (HEAD_DIM // 2)).astype(jnp.float32) / HEAD_DIM
    )
    slot = jnp.arange(8, dtype=jnp.int32)[:, None] ^ ctx
    seat = jnp.array([0, 2, 1, 3], jnp.int32)[None, :] ^ tp
    starts = (slot * (4 * rows) + seat * rows).reshape(32, 1).astype(jnp.float32) * frequency
    inner = jnp.arange(rows, dtype=jnp.float32)[:, None] * frequency
    tables = (jnp.cos(starts), jnp.sin(starts), jnp.cos(inner), jnp.sin(inner))

    own, own_cot = local_call(
        order_kernel, [shaped((2 * rows, width))] * 2, ids, hidden, out_grad, name="order"
    )
    other, other_cot = beside(own, side), beside(own_cot, side)
    core_cot, diag_cot = beside(own_cot, core), beside(other_cot, core)

    w_in_rows = jnp.transpose(w_in, (1, 2, 0)).reshape(2 * units, -1)
    w_out_parts = ring_gather(w_attn_out)
    mlp_parts = ring_gather(jnp.concatenate([low(f32(w_in_rows) * gain_two), w_mlp_out], axis=0))
    w_qkv_parts = ring_gather(low(f32(w_qkv_rows) * gain_one[:, None]))
    mlp_all = jnp.concatenate(mlp_parts, axis=1)
    w_in_all, w_mlp_all = mlp_all[: 2 * units], mlp_all[2 * units :]

    per = 4 * rows
    made = local_call(
        forward_kernel,
        [shaped((per // 2, 128))] * 8
        + [
            shaped((8, per, 128)),
            shaped((8 * per, HEAD_DIM)),
            shaped((8, per, HEAD_DIM), jnp.float32),
            shaped((8, 8, per), jnp.float32),
        ],
        ids,
        *tokens,
        *heads,
        *tables,
        scratch=[pltpu.VMEM((width, 192), jnp.bfloat16), pltpu.VMEM((8 * per, HEAD_DIM), jnp.bfloat16)],
        flops=2 * 8 * per * (width * 192 + 2 * 8 * per * HEAD_DIM),
        name="attention",
    )
    mixed, saved = made[:8], made[8:]
    got = [mixed[0]] + [across(mixed[k], k) for k in range(1, 8)]
    part_kept, part_sent, att = local_call(
        out_kernel,
        [shaped((per, width)), shaped((per, width)), shaped((2 * per, 256))],
        ids,
        *got,
        *w_out_parts,
        scratch=[pltpu.VMEM((4, 2 * per, HEAD_DIM), jnp.bfloat16)],
        flops=2 * 2 * per * 256 * width,
        name="project",
    )

    def core_sum(kept_part, sent_part):
        return local_call(
            sum_kernel, [shaped((per, width))], ids, kept_part, beside(sent_part, core), name="core_sum"
        )[0]

    mine = core_sum(part_kept, part_sent)
    residual, second_a = local_call(
        second_kernel,
        [shaped((per, width), jnp.float32), shaped((per, width))],
        ids,
        own,
        other,
        mine,
        beside(mine, side),
        name="second_norm",
    )
    second_b = beside(second_a, core)

    def geglu(tokens_half, cot_a, cot_b):
        return local_call(
            mlp_kernel,
            [
                shaped((per, width)),
                shaped((per, width)),
                shaped((per, units)),
                shaped((per, 2 * units)),
            ],
            ids,
            tokens_half,
            cot_a,
            cot_b,
            w_in_all,
            w_mlp_all,
            flops=2 * per * width * units * 6,
            name="geglu",
        )

    result_a, back_a, act_a, grad_a = geglu(second_a, own_cot, other_cot)
    result_b, back_b, act_b, grad_b = geglu(second_b, core_cot, diag_cot)

    mine = core_sum(back_a, back_b)
    grad_one, attn_a = local_call(
        third_kernel,
        [shaped((2 * rows, width), jnp.float32), shaped((per, width))],
        ids,
        own_cot,
        other_cot,
        mine,
        beside(mine, side),
        residual,
        name="third_norm",
    )
    attn_b = beside(attn_a, core)
    out_pieces = local_call(
        grad_heads_kernel,
        [shaped((per // 2, 128))] * 8,
        ids,
        attn_a,
        attn_b,
        *w_out_parts,
        flops=2 * 2 * per * 256 * width,
        name="grad_heads",
    )
    grad_mixed = [out_pieces[0]] + [across(out_pieces[k], k) for k in range(1, 8)]

    tall = 3 * units
    cut = tall // 32 * 16
    mlp_blocks = local_call(
        functools.partial(weight_kernel, ((2, 2), (2, 4))),
        [shaped((tall, 128))] * 4 + [shaped((cut, 128)), shaped((tall - cut, 128))] + [shaped((tall, 128))] * 3,
        ids,
        grad_a,
        grad_b,
        second_a,
        second_b,
        act_a,
        act_b,
        own_cot,
        other_cot,
        core_cot,
        diag_cot,
        flops=2 * 2 * per * width * tall,
        name="geglu_weights",
    )
    mlp_sum = ring_sum(mlp_blocks)
    out_blocks = local_call(
        functools.partial(weight_kernel, ((1, 2),)),
        [shaped((256, 128))] * 4 + [shaped((128, 128))] * 2 + [shaped((256, 128))] * 3,
        ids,
        att,
        attn_a,
        attn_b,
        flops=2 * 2 * per * width * 256,
        name="project_weights",
    )
    out_sum = ring_sum(out_blocks)

    mine = core_sum(result_a, result_b)
    (output,) = local_call(
        output_kernel,
        [shaped(hidden.shape)],
        ids,
        residual[: 2 * rows],
        mine[: 2 * rows],
        beside(mine[2 * rows :], side),
        name="output",
    )

    pair_pieces = local_call(
        backward_kernel,
        [shaped((per * 3 // 2, 128))] * 8,
        ids,
        *grad_mixed,
        *saved,
        *tables,
        scratch=[
            pltpu.VMEM((8 * per, HEAD_DIM), jnp.bfloat16),
            pltpu.VMEM((8, per, HEAD_DIM), jnp.bfloat16),
            pltpu.VMEM((8, per, HEAD_DIM), jnp.float32),
            pltpu.VMEM((8 * per, HEAD_DIM), jnp.float32),
            pltpu.VMEM((8 * per, HEAD_DIM), jnp.float32),
        ],
        flops=2 * 8 * per * 5 * 8 * per * HEAD_DIM,
        name="attention_back",
    )
    got = [pair_pieces[0]] + [across(pair_pieces[k], k) for k in range(1, 8)]
    column_pieces = local_call(
        head_grad_kernel,
        [shaped((192, 128))] * 8,
        ids,
        *tokens,
        *pair_pieces,
        scratch=[pltpu.VMEM((192, width), jnp.float32)],
        flops=2 * 8 * per * width * 192,
        name="head_weight_grads",
    )
    columns = [column_pieces[0]] + [across(column_pieces[k], k) for k in range(1, 8)]
    part_kept, part_sent = local_call(
        back_kernel,
        [shaped((per, width))] * 2,
        ids,
        *got,
        *w_qkv_parts,
        scratch=[pltpu.VMEM((3, 4, 2 * per, HEAD_DIM), jnp.bfloat16)],
        flops=2 * 2 * per * width * 768,
        name="qkv_back",
    )
    mine = core_sum(part_kept, part_sent)
    (grad_hidden,) = local_call(
        last_kernel,
        [shaped(hidden.shape, jnp.float32)],
        ids,
        grad_one,
        own,
        mine[: 2 * rows],
        beside(mine[2 * rows :], side),
        name="last_norm",
    )
    grad_qkv, gain_grad_one = local_call(
        columns_kernel,
        [shaped(w_qkv_rows.shape, jnp.float32), shaped((128, 1), jnp.float32)],
        ids,
        *columns,
        gain_one[:, None],
        w_qkv_rows,
        scratch=[pltpu.VMEM((4, 128, 192), jnp.float32)],
        name="qkv_weights",
    )

    def total(parts):
        return f32(parts[0]) + f32(parts[1]) + f32(parts[2])

    mlp_grad = total(mlp_sum)
    grad_in = mlp_grad[: 2 * units]
    gain_grad_two = jnp.sum(grad_in * f32(w_in_rows), axis=0)
    gains = jnp.stack([gain_grad_one[:, 0], gain_grad_two])
    gains = gains + beside(gains, core)
    gains = gains + beside(gains, side)
    return (
        output,
        grad_hidden,
        jnp.transpose(grad_qkv, (1, 0, 2)),
        total(out_sum),
        jnp.transpose((grad_in * gain_two).reshape(2, units, -1), (2, 0, 1)),
        mlp_grad[2 * units :],
        gains[0],
        gains[1],
    )


def layer(hidden, w_qkv, w_attn_out, w_in, w_mlp_out, norm_attn, norm_mlp, out_grad):
    arguments = (hidden, w_qkv, w_attn_out, w_in, w_mlp_out, norm_attn, norm_mlp, out_grad)
    count, micro = lax.axis_size("ctx"), hidden.shape[0]
    one_pair_each = count == micro * (w_qkv.shape[2] // HEAD_DIM) == 8
    if one_pair_each and micro == 2 and lax.axis_size("tp") == 4 and hidden.shape[2] == 128 * count:
        return fast_layer(*arguments)
    return on_device(*arguments)


def solution(mesh):
    return jax.shard_map(
        layer,
        mesh=mesh,
        in_specs=(
            P(None, ("ctx", "tp"), None),
            P("ctx", None, "tp"),
            P("tp", "ctx"),
            P("ctx", None, "tp"),
            P("tp", "ctx"),
            P("ctx"),
            P("ctx"),
            P(None, ("ctx", "tp"), None),
        ),
        out_specs=(
            P(None, ("ctx", "tp"), None),
            P(None, ("ctx", "tp"), None),
            P("ctx", None, "tp"),
            P("tp", "ctx"),
            P("ctx", None, "tp"),
            P("tp", "ctx"),
            P("ctx"),
            P("ctx"),
        ),
        check_vma=False,
    )
```
